128 devices in a mesh: dp: 16 (over x, y_hi, core), hp: 8 (over z, y_lo).
Axes of the slice: x: 4, y: 4 (y_hi: 2, y_lo: 2; y = y_hi * 2 + y_lo), z: 4, core: 2. Of those that a mesh axis runs over, the one named last changes fastest.
Arguments:
- residual: bfloat16 [512, 7168], P('dp', 'hp'), may hold values from -60 to 60
- queries: bfloat16 [512, 128, 192], P('dp', 'hp'), may hold values from -48 to 48
- latent_cache: bfloat16 [512, 512, 576], P('dp'), may hold values from -4 to 4
- new_latent: bfloat16 [512, 576], P('dp'), may hold values from -4 to 4
- lengths: int32 [512], P('dp'), may hold values from 1 to 512, as said below
- w_absorb: bfloat16 [128, 128, 512], P('hp'), may hold values from -0.5 to 0.5
- w_value: bfloat16 [128, 512, 128], P('hp'), may hold values from -0.25 to 0.25
- w_out: bfloat16 [16384, 8, 896], P('hp', None, 'dp'), may hold values from -0.046875 to 0.046875
- norm_gain: bfloat16 [7168], P('hp'), may hold values from 0.099609375 to 1.8984375
- w_gate: bfloat16 [7168, 18432], P('hp', 'dp'), may hold values from -0.0625 to 0.0625
- w_up: bfloat16 [7168, 18432], P('hp', 'dp'), may hold values from -0.0625 to 0.0625
- w_down: bfloat16 [18432, 7168], P('dp', 'hp'), may hold values from -0.046875 to 0.046875
Outputs:
- layer_out: bfloat16 [512, 7168], P('dp', 'hp')
The draws below stay inside these ranges and needn't reach their ends.
Inputs may be any that keep to these rules, and one draw needn't show every extreme that they name: `lengths`: some sample holds all 512 slots in every draw.
All inputs are finite; a program needn't handle non-finite values.
Results may differ from the reference program's by a relative error of at most 0.014.
Values may be sent and summed in bfloat16 or wider, within the bound.
No kernel may reach another device: no remote copies, remote signals or barrier semaphores. Data moves between devices by JAX's collectives and lax.ppermute only.
A program may use at most 128 MiB of HBM per device.

```python
import math
import jax
import jax.numpy as jnp
from jax import lax

D = 7168
FF = 18432
HEADS = 128
NOPE = 128
ROPE = 64
LATENT = 512
VDIM = 128
CTX = 512
SAMPLES = 512
ROWPARTS = 8
DBLK = 896


def attention_parts(key):
    folded = jax.random.fold_in(key, 7)
    subkeys = jax.random.split(folded, 3)
    entry_width = LATENT + ROPE
    cache_rows = jnp.clip(jax.random.normal(subkeys[0], (SAMPLES, CTX, entry_width), jnp.float32), -4.0, 4.0)
    query_rows = jnp.clip(jax.random.normal(subkeys[1], (SAMPLES, HEADS, NOPE + ROPE), jnp.float32), -4.0, 4.0)
    fresh_rows = jnp.clip(jax.random.normal(subkeys[2], (SAMPLES, entry_width), jnp.float32), -4.0, 4.0)
    return (cache_rows, query_rows, fresh_rows)


def draw_latent_cache(key, part):
    return attention_parts(key)[0].astype(jnp.bfloat16)


def draw_queries(key, part):
    return attention_parts(key)[1].astype(jnp.bfloat16)


def draw_new_latent(key, part):
    return attention_parts(key)[2].astype(jnp.bfloat16)


def draw_residual(key, part):
    subkeys = jax.random.split(jax.random.fold_in(key, 23), 2)
    column = jnp.arange(D, dtype=jnp.float32) / D
    spread = jax.random.uniform(subkeys[1], (D,), jnp.float32)
    values = jnp.clip(jax.random.normal(subkeys[0], (SAMPLES, D), jnp.float32), -4.0, 4.0)
    col_scale = 3.0 ** (column - 0.5) * 2.0 ** (spread - 0.5)
    return (values * col_scale[None, :]).astype(jnp.bfloat16)


def draw_lengths(key, part):
    subkeys = jax.random.split(jax.random.fold_in(key, 31), 2)
    drawn = jax.random.randint(subkeys[0], (SAMPLES,), 1, CTX + 1, jnp.int32)
    fullest = jax.random.randint(subkeys[1], (), 0, SAMPLES, jnp.int32)
    return jnp.where(jnp.arange(SAMPLES, dtype=jnp.int32) == fullest, CTX, drawn).astype(jnp.int32)


def block_scale(key, dims, cuts, smallest, top_value):
    level = 1.0
    for position, shards_of in cuts:
        steps = jax.random.uniform(jax.random.fold_in(jax.random.fold_in(key, 6), position), (shards_of,), jnp.float32, smallest / len(cuts), top_value / len(cuts))
        level = level * jnp.repeat(jnp.exp(steps), dims[position] // shards_of).reshape((-1,) + (1,) * (len(dims) - 1 - position))
    return level


def centred(stream_key, extent, width, reach, cuts=(), kind=jnp.bfloat16):
    result = width * jax.random.normal(stream_key, extent, jnp.float32)
    if cuts:
        result = result * block_scale(stream_key, extent, cuts, -0.22, 0.18)
    return jnp.clip(result, -reach, reach).astype(kind)


def setup_inputs(seed: int = 0) -> dict:
    seeds = jax.random.split(jax.random.key(seed), 13)
    return {
        "residual": draw_residual(jax.random.fold_in(seeds[12], 71), 0),
        "queries": draw_queries(jax.random.fold_in(seeds[12], 71), 0),
        "latent_cache": draw_latent_cache(jax.random.fold_in(seeds[12], 71), 0),
        "new_latent": draw_new_latent(jax.random.fold_in(seeds[12], 71), 0),
        "lengths": draw_lengths(jax.random.fold_in(seeds[12], 71), 0),
        "w_absorb": centred(seeds[5], (HEADS, NOPE, LATENT), NOPE ** -0.5, 0.5, ((0, 8),)),
        "w_value": centred(seeds[6], (HEADS, LATENT, VDIM), LATENT ** -0.5, 0.25, ((0, 8),)),
        "w_out": centred(seeds[7], (HEADS * VDIM, ROWPARTS, DBLK), (HEADS * VDIM) ** -0.5, 0.046875, ((0, 8), (2, 16))),
        "norm_gain": jnp.clip(1.0 + 0.18 * jax.random.normal(seeds[8], (D,), jnp.float32), 0.099609375, 1.8984375).astype(jnp.bfloat16),
        "w_gate": centred(seeds[9], (D, FF), D ** -0.5, 0.0625, ((0, 8), (1, 16))),
        "w_up": centred(seeds[10], (D, FF), D ** -0.5, 0.0625, ((0, 8), (1, 16))),
        "w_down": centred(seeds[11], (FF, D), FF ** -0.5, 0.046875, ((0, 16), (1, 8))),
    }


def sample_latent(operands):
    query_full, cache_rows, fresh_row, length = operands
    softmax_scale = 1.0 / math.sqrt(NOPE + ROPE)
    positions = jnp.arange(CTX, dtype=jnp.int32)
    query_wide = query_full.astype(jnp.float32)
    scores = jnp.einsum('hc,lc->hl', query_wide, cache_rows.astype(jnp.float32)) * softmax_scale
    scores = jnp.where(positions[None, :] < length, scores, -1e+30)
    own_score = jnp.einsum('hc,c->h', query_wide, fresh_row.astype(jnp.float32)) * softmax_scale
    peak = jnp.maximum(lax.optimization_barrier(jnp.max(scores, axis=1)), own_score)
    cached_exp = jnp.exp(scores - peak[:, None])
    own_exp = jnp.exp(own_score - peak)
    total = lax.optimization_barrier(jnp.sum(cached_exp, axis=1)) + own_exp
    probs_bf = (cached_exp / total[:, None]).astype(jnp.bfloat16)
    own_prob = (own_exp / total).astype(jnp.bfloat16)
    mixed = jnp.einsum('hl,lc->hc', probs_bf.astype(jnp.float32), cache_rows[:, :LATENT].astype(jnp.float32))
    mixed = mixed + own_prob.astype(jnp.float32)[:, None] * fresh_row[:LATENT].astype(jnp.float32)[None, :]
    return mixed.astype(jnp.bfloat16)

def reference(residual, queries, latent_cache, new_latent, lengths, w_absorb, w_value, w_out, norm_gain, w_gate, w_up, w_down):
    query_latent = jnp.einsum('shn,hnc->shc', queries[:, :, :NOPE].astype(jnp.float32), w_absorb.astype(jnp.float32)).astype(jnp.bfloat16)
    query_full = jnp.concatenate([query_latent, queries[:, :, NOPE:]], axis=2)
    head_latent = lax.map(sample_latent, (query_full, latent_cache, new_latent, lengths))
    head_values = jnp.einsum('shc,hcv->shv', head_latent.astype(jnp.float32), w_value.astype(jnp.float32)).astype(jnp.bfloat16)
    head_values = head_values.reshape(SAMPLES, HEADS * VDIM)
    attention_out = jnp.dot(head_values, w_out.reshape(HEADS * VDIM, D), preferred_element_type=jnp.float32).astype(jnp.bfloat16)
    hidden_state = residual.astype(jnp.float32) + attention_out.astype(jnp.float32)
    row_power = lax.optimization_barrier(jnp.sum(hidden_state * hidden_state, axis=1)) / D
    normed = (hidden_state * lax.rsqrt(row_power + 1e-06)[:, None] * norm_gain.astype(jnp.float32)[None, :]).astype(jnp.bfloat16)
    gate_sum = jnp.dot(normed, w_gate, preferred_element_type=jnp.float32)
    up_sum = jnp.dot(normed, w_up, preferred_element_type=jnp.float32)
    activated = (jax.nn.silu(gate_sum) * up_sum).astype(jnp.bfloat16)
    ffn_out = jnp.dot(activated, w_down, preferred_element_type=jnp.float32)
    return (hidden_state + ffn_out).astype(jnp.bfloat16)
```

```python
import math

import jax
import jax.numpy as jnp
from jax import lax
from jax.sharding import Mesh, PartitionSpec as P

D = 7168
F32 = jnp.float32
BF16 = jnp.bfloat16
DP = ("x", "h", "c")
CHIPS = ("x", "h")
HP = ("z", "l")


def from_everyone(x, axes):
    devices = lax.axis_size(axes)
    return lax.all_to_all(jnp.broadcast_to(x[None], (devices, *x.shape)), axes, 0, 0, tiled=True)


def exchange(x, axes):
    return lax.all_to_all(x, axes, 0, 0, tiled=True)


def dot(a, b, dims):
    return lax.dot_general(a, b, (dims, ((), ())), preferred_element_type=F32)


def other_core(w):
    return lax.ppermute(w, "c", [(0, 1), (1, 0)])


def attention(queries, latent_cache, new_latent, lengths, w_absorb, w_value):
    nope_width = w_absorb.shape[1]
    latent_width = w_absorb.shape[2]
    softmax_scale = 1.0 / math.sqrt(queries.shape[2])
    query_latent = jnp.einsum(
        "shn,hnc->shc", queries[:, :, :nope_width], w_absorb, preferred_element_type=F32
    ).astype(BF16)
    query_full = jnp.concatenate([query_latent, queries[:, :, nope_width:]], axis=2)
    scores = (
        jnp.einsum("shc,slc->shl", query_full, latent_cache, preferred_element_type=F32)
        * softmax_scale
    )
    positions = lax.broadcasted_iota(jnp.int32, (1, 1, latent_cache.shape[1]), 2)
    scores = jnp.where(positions < lengths[:, None, None], scores, -1e30)
    own_score = (
        jnp.einsum("shc,sc->sh", query_full, new_latent, preferred_element_type=F32)
        * softmax_scale
    )
    peak = jnp.maximum(jnp.max(scores, axis=2), own_score)
    cached_exp = jnp.exp(scores - peak[:, :, None])
    own_exp = jnp.exp(own_score - peak)
    total = jnp.sum(cached_exp, axis=2) + own_exp
    probs_bf = (cached_exp / total[:, :, None]).astype(BF16)
    own_prob = (own_exp / total).astype(BF16)
    head_latent = jnp.einsum(
        "shl,slc->shc", probs_bf, latent_cache[:, :, :latent_width], preferred_element_type=F32
    )
    head_latent = head_latent + own_prob.astype(F32)[:, :, None] * new_latent[
        :, None, :latent_width
    ].astype(F32)
    head_latent = head_latent.astype(BF16)
    head_values = jnp.einsum(
        "shc,hcv->shv", head_latent, w_value, preferred_element_type=F32
    ).astype(BF16)
    return head_values.reshape(queries.shape[0], -1)


def on_device(
    residual,
    queries,
    latent_cache,
    new_latent,
    lengths,
    w_absorb,
    w_value,
    w_out,
    norm_gain,
    w_gate,
    w_up,
    w_down,
):
    rows = queries.shape[0]
    width = residual.shape[1]
    core = lax.axis_index("c")
    chip = lax.axis_index(CHIPS)
    outs = (w_out, other_core(w_out))
    gates = (w_gate, other_core(w_gate))
    ups = (w_up, other_core(w_up))
    downs = (w_down, other_core(w_down))

    residual_rows = from_everyone(residual, CHIPS).reshape(-1, width)
    residual_cols = residual_rows.T

    head_values = attention(queries, latent_cache, new_latent, lengths, w_absorb, w_value)
    all_values = from_everyone(head_values, CHIPS).reshape(-1, head_values.shape[1])
    tokens = all_values.shape[0]

    partial = jnp.stack(
        [
            jnp.einsum("tk,kbf->bft", all_values, w, preferred_element_type=F32).astype(BF16)
            for w in outs
        ],
        axis=1,
    )
    arrived = exchange(partial, HP)
    summed = arrived.astype(F32).sum(axis=0).astype(BF16)
    summed = jnp.where(core == 0, summed, summed[::-1])
    attention_cols = from_everyone(summed, CHIPS).reshape(width, tokens)

    hidden_cols = residual_cols.astype(F32) + attention_cols.astype(F32)
    power_part = jnp.sum(hidden_cols * hidden_cols, axis=0).reshape(lax.axis_size(HP), -1)
    scaled = (hidden_cols * norm_gain.astype(F32)[:, None]).astype(BF16)

    sums = [dot(scaled, w, ((0,), (0,))).astype(BF16) for w in gates + ups]
    both = jnp.concatenate(sums, axis=1)
    both = both.reshape(lax.axis_size(HP), -1, both.shape[1])
    both = exchange(both, HP).astype(F32).sum(axis=0)

    row_power = exchange(power_part, HP).sum(axis=0) / D
    both = both * lax.rsqrt(row_power + 1e-06)[:, None]
    gate_sum, up_sum = jnp.split(both, 2, axis=1)
    share = (jax.nn.silu(gate_sum) * up_sum).astype(BF16)
    activated = from_everyone(share, HP).reshape(tokens, -1)

    units = w_down.shape[0]
    ffn = sum(
        dot(activated[:, i * units : (i + 1) * units], w, ((1,), (0,)))
        for i, w in enumerate(downs)
    ).astype(BF16)
    ffn = exchange(ffn.reshape(-1, rows, width), CHIPS).astype(F32).sum(axis=0)

    pick = (
        lax.broadcasted_iota(jnp.int32, (tokens, rows), 0)
        == lax.broadcasted_iota(jnp.int32, (tokens, rows), 1) + chip * rows
    ).astype(BF16)
    own_attention = dot(pick, attention_cols, ((0,), (1,)))
    own_hidden = residual.astype(F32) + own_attention
    return (own_hidden + ffn).astype(BF16)


def solution(mesh):
    fine = Mesh(mesh.devices.reshape(4, 2, 2, 4, 2), ("x", "h", "c", "z", "l"))
    in_specs = (
        P(DP, HP),
        P(DP, HP, None),
        P(DP, None, None),
        P(DP, None),
        P(DP),
        P(HP, None, None),
        P(HP, None, None),
        P(HP, None, DP),
        P(HP),
        P(HP, DP),
        P(HP, DP),
        P(DP, HP),
    )
    return jax.shard_map(
        on_device, mesh=fine, in_specs=in_specs, out_specs=P(DP, HP), check_vma=False
    )
```

```python
import math

import jax
import jax.numpy as jnp
from jax import lax
from jax.experimental import pallas as pl
from jax.experimental.pallas import tpu as pltpu
from jax.sharding import Mesh, PartitionSpec as P


D = 7168
LANES = 128
F32 = jnp.float32
BF16 = jnp.bfloat16
DP = ("x", "h", "c")
CHIPS = ("x", "h")
HP = ("z", "l")


def from_everyone(x, axes):
    devices = lax.axis_size(axes)
    return lax.all_to_all(jnp.broadcast_to(x[None], (devices, *x.shape)), axes, 0, 0, tiled=True)


def exchange(x, axes):
    return lax.all_to_all(x, axes, 0, 0, tiled=True)


def dot(a, b, dims):
    return lax.dot_general(a, b, (dims, ((), ())), preferred_element_type=F32)


def other_core(w):
    return lax.ppermute(w, "c", [(0, 1), (1, 0)])


VMEM = pl.BlockSpec(memory_space=pltpu.VMEM)
HBM = pl.BlockSpec(memory_space=pl.ANY)


def fetch(sources, slots, sems):
    copies = [
        pltpu.make_async_copy(source, slots.at[i], sems.at[i]) for i, source in enumerate(sources)
    ]
    for copy in copies:
        copy.start()
    return copies


def fetch_scratch(sources):
    return [
        pltpu.VMEM((len(sources), *sources[0].shape), sources[0].dtype),
        pltpu.SemaphoreType.DMA((len(sources),)),
    ]


def project(values, weights):
    inner, blocks, cols = weights[0].shape
    rows = values.shape[0]
    weights = [w.transpose(1, 2, 0).reshape(blocks * cols, inner) for w in weights]

    def kernel(values, *refs):
        sources, (out, slots, sems) = refs[: len(weights)], refs[len(weights) :]
        for i, copy in enumerate(fetch(sources, slots, sems)):
            copy.wait()
            part = dot(slots[i], values[...], ((1,), (1,))).astype(BF16)
            for b in range(blocks):
                out[b, i] = part[b * cols : (b + 1) * cols]

    return pl.pallas_call(
        kernel,
        in_specs=[VMEM] + [HBM] * len(weights),
        out_specs=VMEM,
        out_shape=jax.ShapeDtypeStruct((blocks, len(weights), cols, rows), BF16),
        scratch_shapes=fetch_scratch(weights),
        name="project",
    )(values, *weights)


def expand(residual_cols, attention_cols, gain, weights):
    _, tokens = attention_cols.shape
    units = weights[0].shape[1]

    def kernel(residual, attention_out, gain, *refs):
        sources, (out, slots, sems) = refs[: len(weights)], refs[len(weights) :]
        copies = fetch(sources, slots, sems)
        hidden = (residual[...].astype(F32) + attention_out[...].astype(F32)).T
        power = jnp.sum(hidden * hidden, axis=1, keepdims=True)
        high = power.astype(BF16).astype(F32)
        middle = (power - high).astype(BF16).astype(F32)
        low = power - high - middle
        lane = lax.broadcasted_iota(jnp.int32, (tokens, LANES), 1)
        parts = jnp.where(lane == 0, high, jnp.where(lane == 1, middle, low))
        out[:, len(weights) * units :] = jnp.where(lane < 3, parts, 0.0).astype(BF16)
        scaled = (hidden * gain[...]).astype(BF16)
        for i, copy in enumerate(copies):
            copy.wait()
            out[:, i * units : (i + 1) * units] = dot(scaled, slots[i], ((1,), (0,))).astype(BF16)

    return pl.pallas_call(
        kernel,
        in_specs=[VMEM] * 3 + [HBM] * len(weights),
        out_specs=VMEM,
        out_shape=jax.ShapeDtypeStruct((tokens, len(weights) * units + LANES), BF16),
        scratch_shapes=fetch_scratch(weights),
        name="expand",
    )(residual_cols, attention_cols, gain, *weights)


def contract(activated, weights):
    units, width = weights[0].shape

    def kernel(activated, *refs):
        sources, (out, slots, sems) = refs[: len(weights)], refs[len(weights) :]
        total = None
        for i, copy in enumerate(fetch(sources, slots, sems)):
            copy.wait()
            part = dot(activated[:, i * units : (i + 1) * units], slots[i], ((1,), (0,)))
            total = part if total is None else total + part
        out[...] = total.astype(BF16)

    return pl.pallas_call(
        kernel,
        in_specs=[VMEM] + [HBM] * len(weights),
        out_specs=VMEM,
        out_shape=jax.ShapeDtypeStruct((activated.shape[0], width), BF16),
        scratch_shapes=fetch_scratch(weights),
        name="contract",
    )(activated, *weights)


def attention(queries, latent_cache, new_latent, lengths, w_absorb):
    nope_width = w_absorb.shape[1]
    latent_width = w_absorb.shape[2]
    softmax_scale = 1.0 / math.sqrt(queries.shape[2])
    query_latent = jnp.einsum(
        "shn,hnc->shc", queries[:, :, :nope_width], w_absorb, preferred_element_type=F32
    ).astype(BF16)
    query_full = jnp.concatenate([query_latent, queries[:, :, nope_width:]], axis=2)
    scores = (
        jnp.einsum("shc,slc->shl", query_full, latent_cache, preferred_element_type=F32)
        * softmax_scale
    )
    positions = lax.broadcasted_iota(jnp.int32, (1, 1, latent_cache.shape[1]), 2)
    scores = jnp.where(positions < lengths[:, None, None], scores, -1e30)
    own_score = (
        jnp.einsum("shc,sc->sh", query_full, new_latent, preferred_element_type=F32)
        * softmax_scale
    )
    peak = jnp.maximum(jnp.max(scores, axis=2), own_score)
    cached_exp = jnp.exp(scores - peak[:, :, None])
    own_exp = jnp.exp(own_score - peak)
    total = jnp.sum(cached_exp, axis=2) + own_exp
    probs_bf = (cached_exp / total[:, :, None]).astype(BF16)
    own_prob = (own_exp / total).astype(BF16)
    head_latent = jnp.einsum(
        "shl,slc->shc", probs_bf, latent_cache[:, :, :latent_width], preferred_element_type=F32
    )
    head_latent = head_latent + own_prob.astype(F32)[:, :, None] * new_latent[
        :, None, :latent_width
    ].astype(F32)
    return head_latent.astype(BF16)


def layer(
    residual,
    queries,
    latent_cache,
    new_latent,
    lengths,
    w_absorb,
    w_value,
    w_out,
    norm_gain,
    w_gate,
    w_up,
    w_down,
):
    rows = queries.shape[0]
    width = residual.shape[1]
    core = lax.axis_index("c")
    chip = lax.axis_index(CHIPS)
    w_out_other = other_core(w_out)
    w_gate_other = other_core(w_gate)
    w_up_other = other_core(w_up)
    w_down_other = other_core(w_down)
    residual_rows = from_everyone(residual, CHIPS).reshape(-1, width)

    head_latent = attention(queries, latent_cache, new_latent, lengths, w_absorb)
    head_latent, residual_rows, w_out_other = lax.optimization_barrier(
        (head_latent, residual_rows, w_out_other)
    )
    head_values = jnp.einsum("shc,hcv->shv", head_latent, w_value, preferred_element_type=F32)
    head_values = head_values.astype(BF16).reshape(rows, -1)
    all_values = from_everyone(head_values, CHIPS).reshape(-1, head_values.shape[1])
    residual_cols = residual_rows.T
    all_values, residual_cols, w_gate_other, w_up_other, w_down_other = lax.optimization_barrier(
        (all_values, residual_cols, w_gate_other, w_up_other, w_down_other)
    )
    tokens = all_values.shape[0]

    partial = project(all_values, (w_out, w_out_other))
    arrived = exchange(partial, HP)
    summed = arrived.astype(F32).sum(axis=0).astype(BF16)
    summed = jnp.where(core == 0, summed, summed[::-1])
    attention_cols = from_everyone(summed, CHIPS).reshape(width, tokens)

    both = expand(
        residual_cols,
        attention_cols,
        norm_gain.astype(F32)[None, :],
        (w_gate, w_gate_other, w_up, w_up_other),
    )
    both = exchange(both.reshape(lax.axis_size(HP), -1, both.shape[1]), HP)
    both = both.astype(F32).sum(axis=0)
    units = both.shape[1] // 2 - LANES // 2
    row_power = jnp.sum(both[:, 2 * units :], axis=1, keepdims=True) / D
    factor = lax.rsqrt(row_power + 1e-06)
    gate_sum = both[:, :units] * factor
    up_sum = both[:, units : 2 * units] * factor
    share = (jax.nn.silu(gate_sum) * up_sum).astype(BF16)
    activated = from_everyone(share, HP).reshape(tokens, -1)

    ffn = contract(activated, (w_down, w_down_other))
    ffn = exchange(ffn.reshape(-1, rows, width), CHIPS).astype(F32).sum(axis=0)

    pick = (
        lax.broadcasted_iota(jnp.int32, (tokens, rows), 0)
        == lax.broadcasted_iota(jnp.int32, (tokens, rows), 1) + chip * rows
    ).astype(BF16)
    own_attention = dot(pick, attention_cols, ((0,), (1,)))
    own_hidden = residual.astype(F32) + own_attention
    return (own_hidden + ffn).astype(BF16)


def solution(mesh):
    fine = Mesh(mesh.devices.reshape(4, 2, 2, 4, 2), ("x", "h", "c", "z", "l"))
    in_specs = (
        P(DP, HP),
        P(DP, HP, None),
        P(DP, None, None),
        P(DP, None),
        P(DP),
        P(HP, None, None),
        P(HP, None, None),
        P(HP, None, DP),
        P(HP),
        P(HP, DP),
        P(HP, DP),
        P(DP, HP),
    )
    return jax.shard_map(layer, mesh=fine, in_specs=in_specs, out_specs=P(DP, HP), check_vma=False)
```

```python
import functools
import math

import jax
import jax.numpy as jnp
from jax import lax
from jax.experimental import pallas as pl
from jax.experimental.pallas import tpu as pltpu
from jax.sharding import Mesh, PartitionSpec as P


D = 7168
LANES = 128
GROUP = 8
F32 = jnp.float32
BF16 = jnp.bfloat16
DP = ("x", "h", "c")
CHIPS = ("x", "h")
HP = ("z", "l")


def from_everyone(x, axes):
    devices = lax.axis_size(axes)
    return lax.all_to_all(jnp.broadcast_to(x[None], (devices, *x.shape)), axes, 0, 0, tiled=True)


def exchange(x, axes):
    return lax.all_to_all(x, axes, 0, 0, tiled=True)


def dot(a, b, dims):
    return lax.dot_general(a, b, (dims, ((), ())), preferred_element_type=F32)


def other_core(w):
    return lax.ppermute(w, "c", [(0, 1), (1, 0)])


VMEM = pl.BlockSpec(memory_space=pltpu.VMEM)
HBM = pl.BlockSpec(memory_space=pl.ANY)


def expand(places, residuals, attention_cols, gain, weights):
    width, tokens = attention_cols.shape
    units = weights[0].shape[1]
    steps, sides, rows = len(residuals), *residuals[0].shape[:2]

    def kernel(places, attention_out, gain, *refs):
        pieces, sources = refs[:steps], refs[steps : steps + len(weights)]
        out, ready, slots, sums, power_slot, sems = refs[steps + len(weights) :]

        def copy(i, source, target):
            return pltpu.make_async_copy(source, target, sems.at[i])

        first = [copy(i, piece, ready.at[i]) for i, piece in enumerate(pieces)]
        second = [copy(steps + i, w, slots.at[i]) for i, w in enumerate(sources)]
        for c in first + second:
            c.start()
        across = attention_out[...].T.astype(F32)
        for c in first:
            c.wait()
        blocks = []
        for x in range(steps):
            for h in range(sides):
                there = ready[
                    lax.rem(x - places[0] + steps, steps), lax.rem(h - places[1] + sides, sides)
                ]
                at = (x * sides + h) * rows
                blocks.append(there.astype(F32) + across[at : at + rows])
        hidden = jnp.concatenate(blocks, axis=0)
        power = jnp.sum(hidden * hidden, axis=1, keepdims=True)
        high = power.astype(BF16).astype(F32)
        middle = (power - high).astype(BF16).astype(F32)
        low = power - high - middle
        lane = lax.broadcasted_iota(jnp.int32, (tokens, LANES), 1)
        parts = jnp.where(lane == 0, high, jnp.where(lane == 1, middle, low))
        power_slot[...] = jnp.where(lane < 3, parts, 0.0).astype(BF16)
        base = steps + len(weights)
        last = [copy(base, power_slot, out.at[:, len(weights) * units :])]
        last[0].start()
        scaled = (hidden * gain[...]).astype(BF16)
        for i, c in enumerate(second):
            c.wait()
            sums[i] = dot(scaled, slots[i], ((1,), (0,))).astype(BF16)
            last.append(copy(base + 1 + i, sums.at[i], out.at[:, i * units : (i + 1) * units]))
            last[-1].start()
        for c in last:
            c.wait()

    return pl.pallas_call(
        kernel,
        in_specs=[pl.BlockSpec(memory_space=pltpu.SMEM), VMEM, VMEM]
        + [HBM] * (steps + len(weights)),
        out_specs=HBM,
        out_shape=jax.ShapeDtypeStruct((tokens, len(weights) * units + LANES), BF16),
        scratch_shapes=[
            pltpu.VMEM((steps, sides, rows, width), BF16),
            pltpu.VMEM((len(weights), width, units), BF16),
            pltpu.VMEM((len(weights), tokens, units), BF16),
            pltpu.VMEM((tokens, LANES), BF16),
            pltpu.SemaphoreType.DMA((steps + 2 * len(weights) + 1,)),
        ],
        name="expand",
    )(places, attention_cols, gain, *residuals, *weights)


def attend(lengths, query_full, new_latent, cache_cols, latent_width, softmax_scale):
    samples, heads, entry = query_full.shape
    slots = cache_cols.shape[2]
    blocks = slots // LANES
    groups = samples // GROUP

    def kernel(lengths, query, new, cache, out, buf, fresh, order, sems):
        def live(s):
            return lax.div(lengths[s] + (LANES - 1), LANES)

        def tally(s, counts):
            return tuple(c + (live(s) == k + 1).astype(jnp.int32) for k, c in enumerate(counts))

        counts = lax.fori_loop(0, samples, tally, (jnp.int32(0),) * blocks)
        ends = [jnp.int32(0)]
        for c in counts[:-1]:
            ends.append(ends[-1] + c)

        def place(s, ends):
            at = ends[0]
            for k in range(1, blocks):
                at = jnp.where(live(s) == k + 1, ends[k], at)
            order[at] = s
            return tally(s, ends)

        lax.fori_loop(0, samples, place, tuple(ends))

        def by_size(i, act):
            last = live(order[i * GROUP + GROUP - 1])
            for k in range(1, blocks + 1):
                pl.when(last == k)(functools.partial(act, i, k * LANES))

        def copies(act, i, size):
            for g in range(GROUP):
                slot = lax.rem(i, 2) * GROUP + g
                act(
                    pltpu.make_async_copy(
                        cache.at[order[i * GROUP + g], :, :size],
                        buf.at[slot, :, :size],
                        sems.at[slot],
                    )
                )

        start = functools.partial(copies, lambda copy: copy.start())
        wait = functools.partial(copies, lambda copy: copy.wait())
        by_size(0, start)
        by_size(1, start)
        for s in range(samples):
            fresh[s] = new[s : s + 1, :].astype(F32)

        def mix(i, size):
            half = lax.rem(i, 2) * GROUP
            scores, own = [], []
            for g in range(GROUP):
                s = order[i * GROUP + g]
                q = query[s]
                part = dot(q, buf[half + g, :, :size], ((1,), (0,))) * softmax_scale
                positions = lax.broadcasted_iota(jnp.int32, part.shape, 1)
                scores.append(jnp.where(positions < lengths[s], part, -1e30))
                own.append(jnp.sum(q.astype(F32) * fresh[s], axis=1, keepdims=True))
            scores = jnp.concatenate(scores, axis=0)
            own = jnp.concatenate(own, axis=0) * softmax_scale
            peak = jnp.maximum(jnp.max(scores, axis=1, keepdims=True), own)
            cached_exp = jnp.exp(scores - peak)
            own_exp = jnp.exp(own - peak)
            total = jnp.sum(cached_exp, axis=1, keepdims=True) + own_exp
            probs = (cached_exp / total).astype(BF16)
            own_prob = (own_exp / total).astype(BF16).astype(F32)
            for g in range(GROUP):
                s = order[i * GROUP + g]
                mine = slice(g * heads, (g + 1) * heads)
                values = buf[half + g, :latent_width, :size]
                mixed = dot(values, probs[mine], ((1,), (1,))).T
                out[s] = (mixed + own_prob[mine] * fresh[s][:, :latent_width]).astype(BF16)

        def step(i, carry):
            by_size(i, wait)
            by_size(i, mix)

            @pl.when(i + 2 < groups)
            def _():
                by_size(i + 2, start)

            return carry

        lax.fori_loop(0, groups, step, 0)

    return pl.pallas_call(
        kernel,
        in_specs=[pl.BlockSpec(memory_space=pltpu.SMEM), VMEM, VMEM, HBM],
        out_specs=VMEM,
        out_shape=jax.ShapeDtypeStruct((samples, heads, latent_width), BF16),
        scratch_shapes=[
            pltpu.VMEM((2 * GROUP, entry, slots), BF16),
            pltpu.VMEM((samples, 1, entry), F32),
            pltpu.SMEM((samples,), jnp.int32),
            pltpu.SemaphoreType.DMA((2 * GROUP,)),
        ],
        name="attend",
    )(lengths, query_full, new_latent, cache_cols)


def attention(queries, latent_cache, new_latent, lengths, w_absorb):
    nope_width = w_absorb.shape[1]
    query_latent = jnp.einsum(
        "shn,hnc->shc", queries[:, :, :nope_width], w_absorb, preferred_element_type=F32
    ).astype(BF16)
    query_full = jnp.concatenate([query_latent, queries[:, :, nope_width:]], axis=2)
    return attend(
        lengths,
        query_full,
        new_latent,
        latent_cache.swapaxes(1, 2),
        w_absorb.shape[2],
        1.0 / math.sqrt(queries.shape[2]),
    )


def layer(
    residual,
    queries,
    latent_cache,
    new_latent,
    lengths,
    w_absorb,
    w_value,
    w_out,
    norm_gain,
    w_gate,
    w_up,
    w_down,
):
    rows = queries.shape[0]
    width = residual.shape[1]
    core = lax.axis_index("c")
    chip = lax.axis_index(CHIPS)
    w_out_other = other_core(w_out)
    w_gate_other = other_core(w_gate)
    w_up_other = other_core(w_up)
    w_down_other = other_core(w_down)

    head_latent = attention(queries, latent_cache, new_latent, lengths, w_absorb)
    head_latent, w_out_other = lax.optimization_barrier((head_latent, w_out_other))
    head_values = jnp.einsum("shc,hcv->shv", head_latent, w_value, preferred_element_type=F32)
    head_values = head_values.astype(BF16).reshape(rows, -1)
    all_values = from_everyone(head_values, CHIPS).reshape(-1, head_values.shape[1])
    across = lax.ppermute(residual, "h", [(0, 1), (1, 0)])
    all_values, across, w_gate_other, w_up_other, w_down_other = lax.optimization_barrier(
        (all_values, across, w_gate_other, w_up_other, w_down_other)
    )
    tokens = all_values.shape[0]

    partial = jnp.stack(
        [
            jnp.einsum("tk,kbf->bft", all_values, w, preferred_element_type=F32).astype(BF16)
            for w in (w_out, w_out_other)
        ],
        axis=1,
    )
    arrived = exchange(partial, HP)
    both_rows = jnp.stack([residual, across])
    steps = lax.axis_size("x")
    residuals = [both_rows] + [
        lax.ppermute(both_rows, "x", [((i + step) % steps, i) for i in range(steps)])
        for step in range(1, steps)
    ]
    arrived, *residuals = lax.optimization_barrier((arrived, *residuals))
    summed = arrived.astype(F32).sum(axis=0).astype(BF16)
    summed = jnp.where(core == 0, summed, summed[::-1])
    attention_cols = from_everyone(summed, CHIPS).reshape(width, tokens)

    both = expand(
        jnp.stack([lax.axis_index("x"), lax.axis_index("h")]),
        residuals,
        attention_cols,
        norm_gain.astype(F32)[None, :],
        (w_gate, w_gate_other, w_up, w_up_other),
    )
    both = exchange(both.reshape(lax.axis_size(HP), -1, both.shape[1]), HP)
    both = both.astype(F32).sum(axis=0)
    units = both.shape[1] // 2 - LANES // 2
    row_power = jnp.sum(both[:, 2 * units :], axis=1, keepdims=True) / D
    factor = lax.rsqrt(row_power + 1e-06)
    gate_sum = both[:, :units] * factor
    up_sum = both[:, units : 2 * units] * factor
    share = (jax.nn.silu(gate_sum) * up_sum).astype(BF16)
    activated = from_everyone(share, HP).reshape(tokens, -1)

    own_units = w_down.shape[0]
    ffn = sum(
        dot(activated[:, i * own_units : (i + 1) * own_units], w, ((1,), (0,)))
        for i, w in enumerate((w_down, w_down_other))
    ).astype(BF16)
    ffn = exchange(ffn.reshape(-1, rows, width), CHIPS).astype(F32).sum(axis=0)

    pick = (
        lax.broadcasted_iota(jnp.int32, (tokens, rows), 0)
        == lax.broadcasted_iota(jnp.int32, (tokens, rows), 1) + chip * rows
    ).astype(BF16)
    own_attention = dot(pick, attention_cols, ((0,), (1,)))
    own_hidden = residual.astype(F32) + own_attention
    return (own_hidden + ffn).astype(BF16)


def solution(mesh):
    fine = Mesh(mesh.devices.reshape(4, 2, 2, 4, 2), ("x", "h", "c", "z", "l"))
    in_specs = (
        P(DP, HP),
        P(DP, HP, None),
        P(DP, None, None),
        P(DP, None),
        P(DP),
        P(HP, None, None),
        P(HP, None, None),
        P(HP, None, DP),
        P(HP),
        P(HP, DP),
        P(HP, DP),
        P(DP, HP),
    )
    return jax.shard_map(layer, mesh=fine, in_specs=in_specs, out_specs=P(DP, HP), check_vma=False)
```

```python
import functools
import math

import jax
import jax.numpy as jnp
from jax import lax
from jax.experimental import pallas as pl
from jax.experimental.pallas import tpu as pltpu
from jax.sharding import Mesh, PartitionSpec as P


D = 7168
LANES = 128
GROUP = 8
F32 = jnp.float32
BF16 = jnp.bfloat16
DP = ("x", "h", "c")
CHIPS = ("x", "h")
HP = ("z", "l")


def from_everyone(x, axes):
    devices = lax.axis_size(axes)
    return lax.all_to_all(jnp.broadcast_to(x[None], (devices, *x.shape)), axes, 0, 0, tiled=True)


def exchange(x, axes):
    return lax.all_to_all(x, axes, 0, 0, tiled=True)


def dot(a, b, dims):
    return lax.dot_general(a, b, (dims, ((), ())), preferred_element_type=F32)


def other_core(w):
    return lax.ppermute(w, "c", [(0, 1), (1, 0)])


VMEM = pl.BlockSpec(memory_space=pltpu.VMEM)
HBM = pl.BlockSpec(memory_space=pl.ANY)


def expand(places, residuals, attention_cols, gain, weights):
    width, tokens = attention_cols.shape
    units = weights[0].shape[1]
    steps, sides, rows = len(residuals), *residuals[0].shape[:2]

    def kernel(places, attention_out, gain, *refs):
        pieces, sources = refs[:steps], refs[steps : steps + len(weights)]
        out, ready, across_slot, slots, sums, power_slot, sems = refs[steps + len(weights) :]

        def copy(i, source, target):
            return pltpu.make_async_copy(source, target, sems.at[i])

        first = [copy(i, piece, ready.at[i]) for i, piece in enumerate(pieces)]
        first.append(copy(steps, attention_out, across_slot))
        second = [
            copy(steps + 1 + 2 * i + j, w.at[half], slots.at[i, half])
            for i, w in enumerate(sources)
            for j, half in enumerate((slice(0, width // 2), slice(width // 2, width)))
        ]
        for c in first + second[:4]:
            c.start()
        first.pop().wait()
        across = across_slot[...].T.astype(F32)
        for c in first:
            c.wait()
        blocks = []
        for x in range(steps):
            for h in range(sides):
                there = ready[
                    lax.rem(x - places[0] + steps, steps), lax.rem(h - places[1] + sides, sides)
                ]
                at = (x * sides + h) * rows
                blocks.append(there.astype(F32) + across[at : at + rows])
        hidden = jnp.concatenate(blocks, axis=0)
        power = jnp.sum(hidden * hidden, axis=1, keepdims=True)
        high = power.astype(BF16).astype(F32)
        middle = (power - high).astype(BF16).astype(F32)
        low = power - high - middle
        lane = lax.broadcasted_iota(jnp.int32, (tokens, LANES), 1)
        parts = jnp.where(lane == 0, high, jnp.where(lane == 1, middle, low))
        power_slot[...] = jnp.where(lane < 3, parts, 0.0).astype(BF16)
        base = steps + 1 + 2 * len(weights)
        last = [copy(base, power_slot, out.at[:, len(weights) * units :])]
        last[0].start()
        scaled = (hidden * gain[...]).astype(BF16)
        for i in range(len(weights)):
            for c in second[2 * i : 2 * i + 2]:
                c.wait()
            for c in second[2 * i + 4 : 2 * i + 6]:
                c.start()
            sums[i] = dot(scaled, slots[i], ((1,), (0,))).astype(BF16)
            last.append(copy(base + 1 + i, sums.at[i], out.at[:, i * units : (i + 1) * units]))
            last[-1].start()
        for c in last:
            c.wait()

    return pl.pallas_call(
        kernel,
        in_specs=[pl.BlockSpec(memory_space=pltpu.SMEM), HBM, VMEM]
        + [HBM] * (steps + len(weights)),
        out_specs=HBM,
        out_shape=jax.ShapeDtypeStruct((tokens, len(weights) * units + LANES), BF16),
        scratch_shapes=[
            pltpu.VMEM((steps, sides, rows, width), BF16),
            pltpu.VMEM((width, tokens), BF16),
            pltpu.VMEM((len(weights), width, units), BF16),
            pltpu.VMEM((len(weights), tokens, units), BF16),
            pltpu.VMEM((tokens, LANES), BF16),
            pltpu.SemaphoreType.DMA((steps + 2 + 3 * len(weights),)),
        ],
        name="expand",
    )(places, attention_cols, gain, *residuals, *weights)


def attend(lengths, query_latent, queries, new_latent, cache_cols, w_value, copies_out):
    samples, heads, latent_width = query_latent.shape
    entry, slots = cache_cols.shape[1:]
    value_width = w_value.shape[2]
    nope_width = queries.shape[2] - (entry - latent_width)
    softmax_scale = 1.0 / math.sqrt(queries.shape[2])
    blocks = slots // LANES
    groups = samples // GROUP

    def kernel(
        lengths, latent, query, new, cache, w, out, buf, fresh, mixed, w_slot, values, order, sems, w_sem
    ):
        def live(s):
            return lax.div(lengths[s] + (LANES - 1), LANES)

        def tally(s, counts):
            return tuple(c + (live(s) == k + 1).astype(jnp.int32) for k, c in enumerate(counts))

        counts = lax.fori_loop(0, samples, tally, (jnp.int32(0),) * blocks)
        ends = [jnp.int32(0)]
        for c in counts[:-1]:
            ends.append(ends[-1] + c)

        def place(s, ends):
            at = ends[0]
            for k in range(1, blocks):
                at = jnp.where(live(s) == k + 1, ends[k], at)
            order[at] = s
            return tally(s, ends)

        lax.fori_loop(0, samples, place, tuple(ends))

        def by_size(i, act):
            last = live(order[i * GROUP + GROUP - 1])
            for k in range(1, blocks + 1):
                pl.when(last == k)(functools.partial(act, i, k * LANES))

        def copies(act, i, size):
            for g in range(GROUP):
                slot = lax.rem(i, 2) * GROUP + g
                act(
                    pltpu.make_async_copy(
                        cache.at[order[i * GROUP + g], :, :size],
                        buf.at[slot, :, :size],
                        sems.at[slot],
                    )
                )

        start = functools.partial(copies, lambda copy: copy.start())
        wait = functools.partial(copies, lambda copy: copy.wait())
        by_size(0, start)
        by_size(1, start)
        w_copy = pltpu.make_async_copy(w, w_slot, w_sem.at[0])
        w_copy.start()
        for s in range(samples):
            fresh[s] = new[s : s + 1, :].astype(F32)

        def mix(i, size):
            half = lax.rem(i, 2) * GROUP
            scores, own = [], []
            for g in range(GROUP):
                s = order[i * GROUP + g]
                q = latent[s]
                turned = query[s][:, nope_width:]
                part = dot(q, buf[half + g, :latent_width, :size], ((1,), (0,)))
                part = part + dot(turned, buf[half + g, latent_width:, :size], ((1,), (0,)))
                part = part * softmax_scale
                positions = lax.broadcasted_iota(jnp.int32, part.shape, 1)
                scores.append(jnp.where(positions < lengths[s], part, -1e30))
                fresh_row = fresh[s]
                own.append(
                    jnp.sum(q.astype(F32) * fresh_row[:, :latent_width], axis=1, keepdims=True)
                    + jnp.sum(
                        turned.astype(F32) * fresh_row[:, latent_width:], axis=1, keepdims=True
                    )
                )
            scores = jnp.concatenate(scores, axis=0)
            own = jnp.concatenate(own, axis=0) * softmax_scale
            peak = jnp.maximum(jnp.max(scores, axis=1, keepdims=True), own)
            cached_exp = jnp.exp(scores - peak)
            own_exp = jnp.exp(own - peak)
            total = jnp.sum(cached_exp, axis=1, keepdims=True) + own_exp
            probs = (cached_exp / total).astype(BF16)
            own_prob = (own_exp / total).astype(BF16).astype(F32)
            for g in range(GROUP):
                s = order[i * GROUP + g]
                mine = slice(g * heads, (g + 1) * heads)
                kept = buf[half + g, :latent_width, :size]
                sums = dot(kept, probs[mine], ((1,), (1,))).T
                mixed[:, i, g, :] = sums + own_prob[mine] * fresh[s][:, :latent_width]

        def step(i, carry):
            by_size(i, wait)
            by_size(i, mix)

            @pl.when(i + 2 < groups)
            def _():
                by_size(i + 2, start)

            return carry

        lax.fori_loop(0, groups, step, 0)

        row = lax.broadcasted_iota(jnp.int32, (samples, samples), 0)
        col = lax.broadcasted_iota(jnp.int32, (samples, samples), 1)
        source = jnp.zeros((samples, samples), jnp.int32)
        for p in range(samples):
            source = jnp.where(col == p, order[p], source)
        back = (source == row).astype(BF16)
        w_copy.wait()
        heads_values = [
            dot(mixed[h].reshape(samples, latent_width).astype(BF16), w_slot[h], ((1,), (0,)))
            for h in range(heads)
        ]
        sorted_values = jnp.concatenate(heads_values, axis=1).astype(BF16)
        values[...] = dot(back, sorted_values, ((1,), (0,))).astype(BF16)
        last = [
            pltpu.make_async_copy(values, out.at[i], sems.at[i]) for i in range(copies_out)
        ]
        for c in last:
            c.start()
        for c in last:
            c.wait()

    return pl.pallas_call(
        kernel,
        in_specs=[pl.BlockSpec(memory_space=pltpu.SMEM), VMEM, VMEM, VMEM, HBM, HBM],
        out_specs=HBM,
        out_shape=jax.ShapeDtypeStruct((copies_out, samples, heads * value_width), BF16),
        scratch_shapes=[
            pltpu.VMEM((2 * GROUP, entry, slots), BF16),
            pltpu.VMEM((samples, 1, entry), F32),
            pltpu.VMEM((heads, groups, GROUP, latent_width), F32),
            pltpu.VMEM(w_value.shape, BF16),
            pltpu.VMEM((samples, heads * value_width), BF16),
            pltpu.SMEM((samples,), jnp.int32),
            pltpu.SemaphoreType.DMA((2 * GROUP,)),
            pltpu.SemaphoreType.DMA((1,)),
        ],
        cost_estimate=pl.CostEstimate(
            flops=4 * samples * heads * slots * entry,
            bytes_accessed=2 * samples * slots * entry,
            transcendentals=samples * heads * slots,
        ),
        name="attend",
    )(lengths, query_latent, queries, new_latent, cache_cols, w_value)


def layer(
    residual,
    queries,
    latent_cache,
    new_latent,
    lengths,
    w_absorb,
    w_value,
    w_out,
    norm_gain,
    w_gate,
    w_up,
    w_down,
):
    rows = queries.shape[0]
    width = residual.shape[1]
    core = lax.axis_index("c")
    chip = lax.axis_index(CHIPS)
    w_out_other = other_core(w_out)
    w_gate_other = other_core(w_gate)
    w_up_other = other_core(w_up)
    w_down_other = other_core(w_down)

    query_latent = jnp.einsum(
        "shn,hnc->shc", queries[:, :, : w_absorb.shape[1]], w_absorb, preferred_element_type=F32
    ).astype(BF16)
    head_values = attend(
        lengths,
        query_latent,
        queries,
        new_latent,
        latent_cache.swapaxes(1, 2),
        w_value,
        lax.axis_size(CHIPS),
    )
    head_values, w_out_other = lax.optimization_barrier((head_values, w_out_other))
    w_out_both = jnp.stack([w_out, w_out_other], axis=2)
    all_values = exchange(head_values, CHIPS).reshape(-1, head_values.shape[2])
    across = lax.ppermute(residual, "h", [(0, 1), (1, 0)])
    all_values, across, w_out_both, w_gate_other, w_up_other, w_down_other = (
        lax.optimization_barrier(
            (all_values, across, w_out_both, w_gate_other, w_up_other, w_down_other)
        )
    )
    w_down_both = jnp.concatenate([w_down, w_down_other], axis=0)
    tokens = all_values.shape[0]

    partial = jnp.einsum(
        "tk,kbcf->bcft", all_values, w_out_both, preferred_element_type=F32
    ).astype(BF16)
    arrived = exchange(partial, HP)
    both_rows = jnp.stack([residual, across])
    steps = lax.axis_size("x")
    residuals = [both_rows] + [
        lax.ppermute(both_rows, "x", [((i + step) % steps, i) for i in range(steps)])
        for step in range(1, steps)
    ]
    arrived, w_down_both, *residuals = lax.optimization_barrier(
        (arrived, w_down_both, *residuals)
    )
    summed = arrived.astype(F32).sum(axis=0).astype(BF16)
    summed = jnp.where(core == 0, summed, summed[::-1])
    attention_cols = from_everyone(summed, CHIPS).reshape(width, tokens)

    both = expand(
        jnp.stack([lax.axis_index("x"), lax.axis_index("h")]),
        residuals,
        attention_cols,
        norm_gain.astype(F32)[None, :],
        (w_gate, w_gate_other, w_up, w_up_other),
    )
    both = exchange(both.reshape(lax.axis_size(HP), -1, both.shape[1]), HP)
    both = both.astype(F32).sum(axis=0)
    units = both.shape[1] // 2 - LANES // 2
    row_power = jnp.sum(both[:, 2 * units :], axis=1, keepdims=True) / D
    factor = lax.rsqrt(row_power + 1e-06)
    gate_sum = both[:, :units] * factor
    up_sum = both[:, units : 2 * units] * factor
    share = (jax.nn.silu(gate_sum) * up_sum).astype(BF16)
    activated = from_everyone(share, HP).reshape(tokens, -1)

    ffn = dot(activated, w_down_both, ((1,), (0,))).astype(BF16)
    ffn = exchange(ffn.reshape(-1, rows, width), CHIPS).astype(F32).sum(axis=0)

    pick = (
        lax.broadcasted_iota(jnp.int32, (tokens, rows), 0)
        == lax.broadcasted_iota(jnp.int32, (tokens, rows), 1) + chip * rows
    ).astype(BF16)
    own_attention = dot(pick, attention_cols, ((0,), (1,)))
    own_hidden = residual.astype(F32) + own_attention
    return (own_hidden + ffn).astype(BF16)


def solution(mesh):
    fine = Mesh(mesh.devices.reshape(4, 2, 2, 4, 2), ("x", "h", "c", "z", "l"))
    in_specs = (
        P(DP, HP),
        P(DP, HP, None),
        P(DP, None, None),
        P(DP, None),
        P(DP),
        P(HP, None, None),
        P(HP, None, None),
        P(HP, None, DP),
        P(HP),
        P(HP, DP),
        P(HP, DP),
        P(DP, HP),
    )
    return jax.shard_map(layer, mesh=fine, in_specs=in_specs, out_specs=P(DP, HP), check_vma=False)
```

```python
import functools
import math

import jax
import jax.numpy as jnp
from jax import lax
from jax.experimental import pallas as pl
from jax.experimental.pallas import tpu as pltpu
from jax.sharding import Mesh, PartitionSpec as P


D = 7168
LANES = 128
GROUP = 8
F32 = jnp.float32
BF16 = jnp.bfloat16
DP = ("x", "h", "c")
CHIPS = ("x", "h")
HP = ("z", "l")


def from_everyone(x, axes):
    devices = lax.axis_size(axes)
    return lax.all_to_all(jnp.broadcast_to(x[None], (devices, *x.shape)), axes, 0, 0, tiled=True)


def exchange(x, axes):
    return lax.all_to_all(x, axes, 0, 0, tiled=True)


def dot(a, b, dims):
    return lax.dot_general(a, b, (dims, ((), ())), preferred_element_type=F32)


def other_core(w):
    return lax.ppermute(w, "c", [(0, 1), (1, 0)])


VMEM = pl.BlockSpec(memory_space=pltpu.VMEM)
HBM = pl.BlockSpec(memory_space=pl.ANY)


def expand(places, residuals, attention_cols, gain, weights):
    width, tokens = attention_cols.shape
    units = weights[0].shape[1]
    steps, sides, rows = len(residuals), *residuals[0].shape[:2]

    def kernel(places, attention_out, gain, *refs):
        pieces, sources = refs[:steps], refs[steps : steps + len(weights)]
        out, own, ready, across_slot, whole, slots, sums, power_slot, sems = refs[steps + len(weights) :]

        def copy(i, source, target):
            return pltpu.make_async_copy(source, target, sems.at[i])

        first = [copy(i, piece, ready.at[i]) for i, piece in enumerate(pieces)]
        first.append(copy(steps, attention_out, across_slot))
        second = [
            copy(steps + 1 + 2 * i + j, w.at[half], slots.at[i, half])
            for i, w in enumerate(sources)
            for j, half in enumerate((slice(0, width // 2), slice(width // 2, width)))
        ]
        for c in first + second[:4]:
            c.start()
        first.pop().wait()
        across = across_slot[...].T.astype(F32)
        for c in first:
            c.wait()
        blocks = []
        for x in range(steps):
            for h in range(sides):
                there = ready[
                    lax.rem(x - places[0] + steps, steps), lax.rem(h - places[1] + sides, sides)
                ]
                at = (x * sides + h) * rows
                blocks.append(there.astype(F32) + across[at : at + rows])
        hidden = jnp.concatenate(blocks, axis=0)
        whole[...] = hidden
        own[...] = whole[pl.ds(pl.multiple_of((places[0] * sides + places[1]) * rows, rows), rows)]
        power = jnp.sum(hidden * hidden, axis=1, keepdims=True)
        high = power.astype(BF16).astype(F32)
        middle = (power - high).astype(BF16).astype(F32)
        low = power - high - middle
        lane = lax.broadcasted_iota(jnp.int32, (tokens, LANES), 1)
        parts = jnp.where(lane == 0, high, jnp.where(lane == 1, middle, low))
        power_slot[...] = jnp.where(lane < 3, parts, 0.0).astype(BF16)
        base = steps + 1 + 2 * len(weights)
        last = [copy(base, power_slot, out.at[:, len(weights) * units :])]
        last[0].start()
        scaled = (hidden * gain[...]).astype(BF16)
        for i in range(len(weights)):
            for c in second[2 * i : 2 * i + 2]:
                c.wait()
            for c in second[2 * i + 4 : 2 * i + 6]:
                c.start()
            sums[i] = dot(scaled, slots[i], ((1,), (0,))).astype(BF16)
            last.append(copy(base + 1 + i, sums.at[i], out.at[:, i * units : (i + 1) * units]))
            last[-1].start()
        for c in last:
            c.wait()

    return pl.pallas_call(
        kernel,
        in_specs=[pl.BlockSpec(memory_space=pltpu.SMEM), HBM, VMEM]
        + [HBM] * (steps + len(weights)),
        out_specs=(HBM, VMEM),
        out_shape=(
            jax.ShapeDtypeStruct((tokens, len(weights) * units + LANES), BF16),
            jax.ShapeDtypeStruct((rows, width), F32),
        ),
        scratch_shapes=[
            pltpu.VMEM((steps, sides, rows, width), BF16),
            pltpu.VMEM((width, tokens), BF16),
            pltpu.VMEM((tokens, width), F32),
            pltpu.VMEM((len(weights), width, units), BF16),
            pltpu.VMEM((len(weights), tokens, units), BF16),
            pltpu.VMEM((tokens, LANES), BF16),
            pltpu.SemaphoreType.DMA((steps + 2 + 3 * len(weights),)),
        ],
        name="expand",
    )(places, attention_cols, gain, *residuals, *weights)


def attend(lengths, query_latent, queries, new_latent, cache_cols, w_value, copies_out):
    samples, heads, latent_width = query_latent.shape
    entry, slots = cache_cols.shape[1:]
    value_width = w_value.shape[2]
    nope_width = queries.shape[2] - (entry - latent_width)
    softmax_scale = 1.0 / math.sqrt(queries.shape[2])
    blocks = slots // LANES
    groups = samples // GROUP

    def kernel(
        lengths, latent, query, new, cache, w, out, buf, fresh, mixed, w_slot, values, order, sems, w_sem
    ):
        def live(s):
            return lax.div(lengths[s] + (LANES - 1), LANES)

        def tally(s, counts):
            return tuple(c + (live(s) == k + 1).astype(jnp.int32) for k, c in enumerate(counts))

        counts = lax.fori_loop(0, samples, tally, (jnp.int32(0),) * blocks)
        ends = [jnp.int32(0)]
        for c in counts[:-1]:
            ends.append(ends[-1] + c)

        def place(s, ends):
            at = ends[0]
            for k in range(1, blocks):
                at = jnp.where(live(s) == k + 1, ends[k], at)
            order[at] = s
            return tally(s, ends)

        lax.fori_loop(0, samples, place, tuple(ends))

        def by_size(i, act):
            last = live(order[i * GROUP + GROUP - 1])
            for k in range(1, blocks + 1):
                pl.when(last == k)(functools.partial(act, i, k * LANES))

        def copies(act, i, size):
            for g in range(GROUP):
                slot = lax.rem(i, 2) * GROUP + g
                act(
                    pltpu.make_async_copy(
                        cache.at[order[i * GROUP + g], :, :size],
                        buf.at[slot, :, :size],
                        sems.at[slot],
                    )
                )

        start = functools.partial(copies, lambda copy: copy.start())
        wait = functools.partial(copies, lambda copy: copy.wait())
        by_size(0, start)
        by_size(1, start)
        w_copy = pltpu.make_async_copy(w, w_slot, w_sem.at[0])
        w_copy.start()
        for s in range(samples):
            fresh[s] = new[s : s + 1, :].astype(F32)

        def mix(i, size):
            half = lax.rem(i, 2) * GROUP
            scores, own = [], []
            for g in range(GROUP):
                s = order[i * GROUP + g]
                q = latent[s]
                turned = query[s][:, nope_width:]
                part = dot(q, buf[half + g, :latent_width, :size], ((1,), (0,)))
                part = part + dot(turned, buf[half + g, latent_width:, :size], ((1,), (0,)))
                part = part * softmax_scale
                positions = lax.broadcasted_iota(jnp.int32, part.shape, 1)
                scores.append(jnp.where(positions < lengths[s], part, -1e30))
                fresh_row = fresh[s]
                own.append(
                    jnp.sum(q.astype(F32) * fresh_row[:, :latent_width], axis=1, keepdims=True)
                    + jnp.sum(
                        turned.astype(F32) * fresh_row[:, latent_width:], axis=1, keepdims=True
                    )
                )
            scores = jnp.concatenate(scores, axis=0)
            own = jnp.concatenate(own, axis=0) * softmax_scale
            peak = jnp.maximum(jnp.max(scores, axis=1, keepdims=True), own)
            cached_exp = jnp.exp(scores - peak)
            own_exp = jnp.exp(own - peak)
            total = jnp.sum(cached_exp, axis=1, keepdims=True) + own_exp
            probs = (cached_exp / total).astype(BF16)
            own_prob = (own_exp / total).astype(BF16).astype(F32)
            for g in range(GROUP):
                s = order[i * GROUP + g]
                mine = slice(g * heads, (g + 1) * heads)
                kept = buf[half + g, :latent_width, :size]
                sums = dot(kept, probs[mine], ((1,), (1,))).T
                mixed[:, i, g, :] = sums + own_prob[mine] * fresh[s][:, :latent_width]

        def step(i, carry):
            by_size(i, wait)
            by_size(i, mix)

            @pl.when(i + 2 < groups)
            def _():
                by_size(i + 2, start)

            return carry

        lax.fori_loop(0, groups, step, 0)

        row = lax.broadcasted_iota(jnp.int32, (samples, samples), 0)
        col = lax.broadcasted_iota(jnp.int32, (samples, samples), 1)
        source = jnp.zeros((samples, samples), jnp.int32)
        for p in range(samples):
            source = jnp.where(col == p, order[p], source)
        back = (source == row).astype(BF16)
        w_copy.wait()
        heads_values = [
            dot(mixed[h].reshape(samples, latent_width).astype(BF16), w_slot[h], ((1,), (0,)))
            for h in range(heads)
        ]
        sorted_values = jnp.concatenate(heads_values, axis=1).astype(BF16)
        values[...] = dot(back, sorted_values, ((1,), (0,))).astype(BF16)
        last = [
            pltpu.make_async_copy(values, out.at[i], sems.at[i]) for i in range(copies_out)
        ]
        for c in last:
            c.start()
        for c in last:
            c.wait()

    return pl.pallas_call(
        kernel,
        in_specs=[pl.BlockSpec(memory_space=pltpu.SMEM), VMEM, VMEM, VMEM, HBM, HBM],
        out_specs=HBM,
        out_shape=jax.ShapeDtypeStruct((copies_out, samples, heads * value_width), BF16),
        scratch_shapes=[
            pltpu.VMEM((2 * GROUP, entry, slots), BF16),
            pltpu.VMEM((samples, 1, entry), F32),
            pltpu.VMEM((heads, groups, GROUP, latent_width), F32),
            pltpu.VMEM(w_value.shape, BF16),
            pltpu.VMEM((samples, heads * value_width), BF16),
            pltpu.SMEM((samples,), jnp.int32),
            pltpu.SemaphoreType.DMA((2 * GROUP,)),
            pltpu.SemaphoreType.DMA((1,)),
        ],
        cost_estimate=pl.CostEstimate(
            flops=4 * samples * heads * slots * entry,
            bytes_accessed=2 * samples * slots * entry,
            transcendentals=samples * heads * slots,
        ),
        name="attend",
    )(lengths, query_latent, queries, new_latent, cache_cols, w_value)


def layer(
    residual,
    queries,
    latent_cache,
    new_latent,
    lengths,
    w_absorb,
    w_value,
    w_out,
    norm_gain,
    w_gate,
    w_up,
    w_down,
):
    rows = queries.shape[0]
    width = residual.shape[1]
    core = lax.axis_index("c")
    w_out_other = other_core(w_out)
    w_gate_other = other_core(w_gate)
    w_up_other = other_core(w_up)
    w_down_other = other_core(w_down)

    query_latent = jnp.einsum(
        "shn,hnc->shc", queries[:, :, : w_absorb.shape[1]], w_absorb, preferred_element_type=F32
    ).astype(BF16)
    head_values = attend(
        lengths,
        query_latent,
        queries,
        new_latent,
        latent_cache.swapaxes(1, 2),
        w_value,
        lax.axis_size(CHIPS),
    )
    head_values, w_out_other, w_down_other = lax.optimization_barrier(
        (head_values, w_out_other, w_down_other)
    )
    w_out_both = jnp.stack([w_out, w_out_other], axis=2)
    all_values = exchange(head_values, CHIPS).reshape(-1, head_values.shape[2])
    across = lax.ppermute(residual, "h", [(0, 1), (1, 0)])
    w_down_both = jnp.concatenate([w_down, w_down_other], axis=0)
    gain = norm_gain.astype(F32)[None, :]
    places = jnp.stack([lax.axis_index("x"), lax.axis_index("h")])
    all_values, w_out_both, w_down_both, w_gate_other, w_up_other, gain, places = (
        lax.optimization_barrier(
            (all_values, w_out_both, w_down_both, w_gate_other, w_up_other, gain, places)
        )
    )
    tokens = all_values.shape[0]

    partial = jnp.einsum(
        "tk,kbcf->bcft", all_values, w_out_both, preferred_element_type=F32
    ).astype(BF16)
    arrived = exchange(partial, HP)
    both_rows = jnp.stack([residual, across])
    steps = lax.axis_size("x")
    residuals = [both_rows] + [
        lax.ppermute(both_rows, "x", [((i + step) % steps, i) for i in range(steps)])
        for step in range(1, steps)
    ]
    arrived, *residuals = lax.optimization_barrier((arrived, *residuals))
    summed = arrived.astype(F32).sum(axis=0).astype(BF16)
    summed = jnp.where(core == 0, summed, summed[::-1])
    attention_cols = from_everyone(summed, CHIPS).reshape(width, tokens)

    both, own_hidden = expand(
        places,
        residuals,
        attention_cols,
        gain,
        (w_gate, w_gate_other, w_up, w_up_other),
    )
    both = exchange(both.reshape(lax.axis_size(HP), -1, both.shape[1]), HP)
    both = both.astype(F32).sum(axis=0)
    units = both.shape[1] // 2 - LANES // 2
    row_power = jnp.sum(both[:, 2 * units :], axis=1, keepdims=True) / D
    factor = lax.rsqrt(row_power + 1e-06)
    gate_sum = both[:, :units] * factor
    up_sum = both[:, units : 2 * units] * factor
    share = (jax.nn.silu(gate_sum) * up_sum).astype(BF16)
    activated = from_everyone(share, HP).reshape(tokens, -1)

    ffn = dot(activated, w_down_both, ((1,), (0,))).astype(BF16)
    ffn = exchange(ffn.reshape(-1, rows, width), CHIPS).astype(F32).sum(axis=0)

    return (own_hidden + ffn).astype(BF16)


def solution(mesh):
    fine = Mesh(mesh.devices.reshape(4, 2, 2, 4, 2), ("x", "h", "c", "z", "l"))
    in_specs = (
        P(DP, HP),
        P(DP, HP, None),
        P(DP, None, None),
        P(DP, None),
        P(DP),
        P(HP, None, None),
        P(HP, None, None),
        P(HP, None, DP),
        P(HP),
        P(HP, DP),
        P(HP, DP),
        P(DP, HP),
    )
    return jax.shard_map(layer, mesh=fine, in_specs=in_specs, out_specs=P(DP, HP), check_vma=False)
```
